32 devices in a mesh: fsdp: 8 (over z, y), tensor: 4 (over x, core).
Axes of the slice: x: 2, y: 2, z: 4, core: 2. Of those that a mesh axis runs over, the one named last changes fastest.
Arguments:
- images: bfloat16 [2, 8, 577, 1024], P(None, 'fsdp'), may hold values from -6 to 6
- cotangent: bfloat16 [2, 8, 577, 1024], P(None, 'fsdp'), may hold values from -6 to 6
- ln1_gain: bfloat16 [1024], P(('fsdp', 'tensor')), may hold values from 0.5 to 1.5
- ln1_bias: bfloat16 [1024], P(('fsdp', 'tensor')), may hold values from -3 to 3
- qkv_weight: bfloat16 [1024, 16, 192], P('fsdp', 'tensor'), may hold values from -0.1875 to 0.1875
- qv_bias: bfloat16 [16, 128], P('tensor', 'fsdp'), may hold values from -1.1953125 to 1.1953125
- out_weight: bfloat16 [1024, 1024], P('tensor', 'fsdp'), may hold values from -0.75 to 0.75
- out_bias: bfloat16 [1024], P(('fsdp', 'tensor')), may hold values from -3 to 3
- ln2_gain: bfloat16 [1024], P(('fsdp', 'tensor')), may hold values from 0.5 to 1.5
- ln2_bias: bfloat16 [1024], P(('fsdp', 'tensor')), may hold values from -3 to 3
- up_weight: bfloat16 [1024, 4096], P('fsdp', 'tensor'), may hold values from -0.1875 to 0.1875
- up_bias: bfloat16 [4, 1024], P('tensor', 'fsdp'), may hold values from -3 to 3
- down_weight: bfloat16 [4096, 1024], P('tensor', 'fsdp'), may hold values from -0.09375 to 0.09375
- down_bias: bfloat16 [1024], P(('fsdp', 'tensor')), may hold values from -3 to 3
Outputs:
- activations: bfloat16 [2, 8, 577, 1024], P(None, 'fsdp')
- input_grad: float32 [2, 8, 577, 1024], P(None, 'fsdp')
- ln1_gain_grad: float32 [1024], P(('fsdp', 'tensor'))
- ln1_bias_grad: float32 [1024], P(('fsdp', 'tensor'))
- qkv_weight_grad: float32 [1024, 16, 192], P('fsdp', 'tensor')
- qv_bias_grad: float32 [16, 128], P('tensor', 'fsdp')
- out_weight_grad: float32 [1024, 1024], P('tensor', 'fsdp')
- out_bias_grad: float32 [1024], P(('fsdp', 'tensor'))
- ln2_gain_grad: float32 [1024], P(('fsdp', 'tensor'))
- ln2_bias_grad: float32 [1024], P(('fsdp', 'tensor'))
- up_weight_grad: float32 [1024, 4096], P('fsdp', 'tensor')
- up_bias_grad: float32 [4, 1024], P('tensor', 'fsdp')
- down_weight_grad: float32 [4096, 1024], P('tensor', 'fsdp')
- down_bias_grad: float32 [1024], P(('fsdp', 'tensor'))
The draws below stay inside these ranges and needn't reach their ends.
All inputs are finite; a program needn't handle non-finite values.
Results may differ from the reference program's by a relative error of at most 0.023.
Values may be sent and summed in bfloat16 or wider, within the bound.
No kernel may reach another device: no remote copies, remote signals or barrier semaphores. Data moves between devices by JAX's collectives and lax.ppermute only.
A program may use at most 128 MiB of HBM per device.

```python
import jax
import jax.numpy as jnp
from jax import lax

D = 1024
HEADS = 16
HD = 64
FF = 4096
SEQ = 577
MICRO = 2
IMAGES = 8
N_TENSOR = 4


def block_levels(rng, dims, split, low, high):
    factor_of = 1.0
    for position, shards_of in split:
        draws = jax.random.uniform(jax.random.fold_in(jax.random.fold_in(rng, 6), position), (shards_of,), jnp.float32, low / len(split), high / len(split))
        factor_of = factor_of * jnp.repeat(jnp.exp(draws), dims[position] // shards_of).reshape((-1,) + (1,) * (len(dims) - 1 - position))
    return factor_of


def bell_draw(stream_key, extent, width, reach, pieces=(), kind=jnp.bfloat16):
    result = width * jax.random.normal(stream_key, extent, jnp.float32)
    if pieces:
        result = result * block_levels(stream_key, extent, pieces, -0.22, 0.18)
    return jnp.clip(result, -reach, reach).astype(kind)


def setup_inputs(seed: int = 0) -> dict:
    streams_of = jax.random.split(jax.random.key(seed), 15)
    return {
        "images": bell_draw(streams_of[0], (MICRO, IMAGES, SEQ, D), 1.0, 6.0, ((1, 8),)),
        "cotangent": bell_draw(streams_of[1], (MICRO, IMAGES, SEQ, D), 1.0, 6.0, ((1, 8),)),
        "ln1_gain": jnp.clip(0.5 + 1.0 * jax.random.uniform(streams_of[2], (D,), jnp.float32) ** block_levels(streams_of[2], (D,), ((0, 32),), -0.2, 0.2), 0.5, 1.5).astype(jnp.bfloat16),
        "ln1_bias": bell_draw(streams_of[3], (D,), 0.5, 3.0, ((0, 32),)),
        "qkv_weight": bell_draw(streams_of[4], (D, HEADS, 3 * HD), D ** -0.5, 0.1875, ((0, 8), (1, 4))),
        "qv_bias": bell_draw(streams_of[5], (HEADS, 2 * HD), 0.2, 1.1953125, ((0, 4), (1, 8))),
        "out_weight": bell_draw(streams_of[6], (D, D), (D // 16) ** -0.5, 0.75, ((0, 4), (1, 8))),
        "out_bias": bell_draw(streams_of[7], (D,), 0.5, 3.0, ((0, 32),)),
        "ln2_gain": jnp.clip(0.5 + 1.0 * jax.random.uniform(streams_of[8], (D,), jnp.float32) ** block_levels(streams_of[8], (D,), ((0, 32),), -0.2, 0.2), 0.5, 1.5).astype(jnp.bfloat16),
        "ln2_bias": bell_draw(streams_of[9], (D,), 0.5, 3.0, ((0, 32),)),
        "up_weight": bell_draw(streams_of[10], (D, FF), D ** -0.5, 0.1875, ((0, 8), (1, 4))),
        "up_bias": bell_draw(streams_of[11], (N_TENSOR, FF // N_TENSOR), 0.5, 3.0, ((0, 4), (1, 8))),
        "down_weight": bell_draw(streams_of[12], (FF, D), FF ** -0.5, 0.09375, ((0, 4), (1, 8))),
        "down_bias": bell_draw(streams_of[13], (D,), 0.5, 3.0, ((0, 32),)),
    }


@jax.custom_vjp
def low(v):
    return lax.optimization_barrier(v.astype(jnp.bfloat16)).astype(jnp.float32)

@jax.custom_vjp
def low_back(v):
    return v

def low_keep(v):
    return (low(v), None)

def low_pass(kept, grad):
    return (grad,)

def back_keep(v):
    return (v, None)

def back_low(kept, grad):
    return (low(grad),)
low.defvjp(low_keep, low_pass)
low_back.defvjp(back_keep, back_low)
epsilon = 1e-06
highest = lax.Precision.HIGHEST

def layer_norm(values, scale_vec, shift_vec):
    centred = values - lax.optimization_barrier(jnp.mean(values, axis=-1, keepdims=True))
    spread = lax.optimization_barrier(jnp.mean(centred * centred, axis=-1, keepdims=True))
    return centred * lax.rsqrt(spread + epsilon) * scale_vec + shift_vec

def gelu_exact(values):
    return jax.nn.gelu(values, approximate=False)

def forward(picture, ln1_gain, ln1_bias, qkv_weight, qv_bias, out_weight, out_bias, ln2_gain, ln2_bias, up_weight, up_bias, down_weight, down_bias):
    normed_one = low(layer_norm(picture, ln1_gain, ln1_bias))
    projected = jnp.dot(normed_one, qkv_weight.reshape(D, 3 * D), precision=highest).reshape(SEQ, HEADS, 3 * HD)
    queries = low(low_back(projected[:, :, :HD] + qv_bias[:, :HD]))
    key_rows = low(low_back(projected[:, :, HD:2 * HD]))
    val_rows = low(low_back(projected[:, :, 2 * HD:] + qv_bias[:, HD:]))
    scores = low_back(jnp.einsum('shd,thd->hst', queries, key_rows, precision=highest) * HD ** (-0.5))
    weights_low = low(jax.nn.softmax(scores, axis=-1))
    attended = low(low_back(jnp.einsum('hst,thd->shd', weights_low, val_rows, precision=highest).reshape(SEQ, D)))
    branch = low_back(jnp.dot(attended, out_weight, precision=highest) + out_bias)
    hidden_res = picture + branch
    normed_two = low(layer_norm(hidden_res, ln2_gain, ln2_bias))
    pre_act = low_back(jnp.dot(normed_two, up_weight, precision=highest) + up_bias.reshape(FF))
    activated = low(gelu_exact(pre_act))
    mlp_out = low_back(jnp.dot(activated, down_weight, precision=highest) + down_bias)
    return hidden_res + mlp_out

def reference(images, cotangent, ln1_gain, ln1_bias, qkv_weight, qv_bias, out_weight, out_bias, ln2_gain, ln2_bias, up_weight, up_bias, down_weight, down_bias):
    params = (ln1_gain.astype(jnp.float32), ln1_bias.astype(jnp.float32), qkv_weight.astype(jnp.float32), qv_bias.astype(jnp.float32), out_weight.astype(jnp.float32), out_bias.astype(jnp.float32), ln2_gain.astype(jnp.float32), ln2_bias.astype(jnp.float32), up_weight.astype(jnp.float32), up_bias.astype(jnp.float32), down_weight.astype(jnp.float32), down_bias.astype(jnp.float32))
    flat_images = images.reshape(MICRO * IMAGES, SEQ, D).astype(jnp.float32)
    flat_cot = cotangent.reshape(MICRO * IMAGES, SEQ, D).astype(jnp.float32)

    def one_image(running, pair_item):
        picture, cot_image = pair_item
        result_out, pull_back = jax.vjp(forward, picture, *params)
        gradients = pull_back(cot_image)
        updated = tuple((total_old + fresh for total_old, fresh in zip(running, gradients[1:])))
        return (updated, (result_out.astype(jnp.bfloat16), gradients[0]))
    zeroes = tuple((jnp.zeros_like(member) for member in params))
    totals, stacked = lax.scan(one_image, zeroes, (flat_images, flat_cot))
    activations = stacked[0].reshape(images.shape)
    input_grad = stacked[1].reshape(images.shape)
    return (activations, input_grad, totals[0], totals[1], totals[2], totals[3], totals[4], totals[5], totals[6], totals[7], totals[8], totals[9], totals[10], totals[11])
```

```python
import jax
import jax.numpy as jnp
from jax import lax
from jax.experimental import pallas as pl
from jax.experimental.pallas import tpu as pltpu
from jax.sharding import Mesh, PartitionSpec as P

epsilon = 1e-06
f32 = jnp.float32
bf16 = jnp.bfloat16


def after(value, *tokens):
    return lax.optimization_barrier((value,) + tokens)[0]


def dot(a, b, dims):
    return lax.dot_general(a, b, (dims, ((), ())), preferred_element_type=f32)


def mm(a, b):
    return dot(a, b, ((1,), (0,)))


def mm_nt(a, b):
    return dot(a, b, ((1,), (1,)))


def mm_tn(a, b):
    return dot(a, b, ((0,), (0,)))


class TorusPlan:
    axes = ("z", "y", "x", "c")
    fsdp = ("z", "y")
    tensor = ("x", "c")

    def mesh(self, mesh):
        return Mesh(mesh.devices.reshape(4, 2, 2, 2), self.axes)

    def swap(self, value, axis):
        return lax.ppermute(value, axis, [(0, 1), (1, 0)])

    def from_z(self, value, shift):
        return lax.ppermute(value, "z", [((d + shift) % 4, d) for d in range(4)])

    def micro(self):
        return lax.axis_index("x")

    def stage_z(self, shard):
        return jnp.concatenate([shard] + [self.from_z(shard, s) for s in (1, 2, 3)], axis=0)

    def stage_xy(self, four):
        return self.swap(four, "x"), self.swap(four, "y")

    def stage_diag(self, four, over_x, over_y):
        half = four.shape[0] // 2
        return self.swap(over_x[:half], "y"), self.swap(over_y[half:], "x")

    def join(self, four, over_x, over_y, diag_a, diag_b):
        own = jnp.concatenate([four, over_y], axis=0)
        other = jnp.concatenate([over_x, diag_a, diag_b], axis=0)
        return own, other

    def gather_all(self, shards):
        qkv, out, up, down = shards[1:]
        four_s = self.stage_z(shards[0])
        s_xy = self.stage_xy(four_s)
        small = self.join(four_s, *s_xy, *self.stage_diag(four_s, *s_xy))
        four_q = self.stage_z(qkv)
        q_xy = self.stage_xy(four_q)
        four_o = self.stage_z(after(out, four_q))
        four_u = self.stage_z(after(up, four_q))
        q_diag = self.stage_diag(four_q, *q_xy)
        o_xy = self.stage_xy(after(four_o, *q_xy))
        o_diag = self.stage_diag(four_o, *o_xy)
        four_d = self.stage_z(after(down, four_u))
        u_xy = self.stage_xy(after(four_u, *q_diag))
        u_diag = self.stage_diag(four_u, *u_xy)
        d_xy = self.stage_xy(after(four_d, *u_xy))
        d_diag = self.stage_diag(four_d, *d_xy)
        return (
            small,
            self.join(four_q, *q_xy, *q_diag),
            self.join(four_o, *o_xy, *o_diag),
            self.join(four_u, *u_xy, *u_diag),
            self.join(four_d, *d_xy, *d_diag),
        )

    def scatter(self, d_side, own, other):
        width = d_side.shape[1]
        q, h = width // 4, width // 2
        first = mm_tn(d_side[:, h : h + q], other).astype(bf16)
        second = mm_tn(d_side[:, h + q :], other).astype(bf16)
        first = self.swap(first, "y").astype(f32)
        second = self.swap(second, "x").astype(f32)
        part_x = mm_tn(d_side[:, :h], other) + jnp.pad(first, ((0, q), (0, 0)))
        part_y = mm_tn(d_side[:, h:], own) + jnp.pad(second, ((q, 0), (0, 0)))
        part_x = self.swap(part_x.astype(bf16), "x").astype(f32)
        part_y = self.swap(part_y.astype(bf16), "y").astype(f32)
        total = mm_tn(d_side[:, :h], own) + part_x + part_y
        return self.finish(total)

    def finish(self, total):
        rows = total.shape[0] // 4
        total = total.astype(bf16)
        result = total[:rows].astype(f32)
        for shift in (1, 2, 3):
            piece = total[rows * shift : rows * (shift + 1)]
            result = result + self.from_z(piece, 4 - shift).astype(f32)
        return result

    def scatter_small(self, own, other):
        own, other = own.astype(bf16), other.astype(bf16)
        first = self.swap(other[4:6], "y").astype(f32)
        second = self.swap(other[6:8], "x").astype(f32)
        part_x = other[:4].astype(f32) + jnp.pad(first, ((0, 2), (0, 0)))
        part_y = own[4:].astype(f32) + jnp.pad(second, ((2, 0), (0, 0)))
        part_x = self.swap(part_x.astype(bf16), "x").astype(f32)
        part_y = self.swap(part_y.astype(bf16), "y").astype(f32)
        return self.finish(own[:4].astype(f32) + part_x + part_y)

    def pair_sum(self, part):
        low = part.astype(bf16)
        return low.astype(f32) + self.swap(low, "c").astype(f32)

    def to_abs(self, value):
        value = value.reshape((2, 4) + value.shape[1:])
        value = jnp.where(lax.axis_index("y") == 0, value, value[::-1])
        double = jnp.concatenate([value, value], axis=1)
        value = lax.dynamic_slice_in_dim(double, (4 - lax.axis_index("z")) % 4, 4, 1)
        value = jnp.swapaxes(value, 0, 1)
        return value.reshape((8,) + value.shape[2:])

    def to_rel(self, value):
        value = jnp.swapaxes(value.reshape((4, 2) + value.shape[1:]), 0, 1)
        value = jnp.where(lax.axis_index("y") == 0, value, value[::-1])
        double = jnp.concatenate([value, value], axis=1)
        value = lax.dynamic_slice_in_dim(double, lax.axis_index("z"), 4, 1)
        return value.reshape((8,) + value.shape[2:])

    def pack_small(self, vectors, qv, up):
        mine = jnp.stack(vectors)[:, None]
        theirs = self.swap(mine, "c")
        at_zero = lax.axis_index("c") == 0
        both = jnp.concatenate(
            [jnp.where(at_zero, mine, theirs), jnp.where(at_zero, theirs, mine)], axis=1
        )
        flat = jnp.concatenate([both.reshape(-1), qv.reshape(-1), up.reshape(-1)])
        return flat.reshape(1, -1)

    def unpack_small(self, pair, heads, qv_cols, up_cols):
        own, other = pair
        count = 6 * 64
        at_zero = lax.axis_index("x") == 0
        low = jnp.where(at_zero, own[:, :count], other[:, :count]).reshape(8, 6, 64)
        high = jnp.where(at_zero, other[:, :count], own[:, :count]).reshape(8, 6, 64)
        vectors = jnp.swapaxes(jnp.concatenate([low, high], axis=2), 0, 1).reshape(6, -1)
        qvs, ups = [], []
        for side in (own, other):
            tail = self.to_abs(side[:, count:])
            qv = tail[:, : heads * qv_cols].reshape(8, heads, qv_cols)
            qvs.append(jnp.swapaxes(qv, 0, 1).reshape(heads, 8 * qv_cols))
            ups.append(tail[:, heads * qv_cols :].reshape(-1))
        return list(vectors.astype(f32)), [q.astype(f32) for q in qvs], [u.astype(f32) for u in ups]

    def small_grads(self, vectors, qvs, ups):
        rows = jnp.swapaxes(jnp.stack(vectors).reshape(6, 8, 128), 0, 1)
        at_zero = lax.axis_index("x") == 0
        sides = (
            jnp.where(at_zero, rows[:, :, :64], rows[:, :, 64:]),
            jnp.where(at_zero, rows[:, :, 64:], rows[:, :, :64]),
        )
        packed = []
        heads = qvs[0].shape[0]
        for side, qv, up in zip(sides, qvs, ups):
            qv_rows = jnp.swapaxes(qv.reshape(heads, 8, -1), 0, 1).reshape(8, -1)
            tail = self.to_rel(jnp.concatenate([qv_rows, up.reshape(8, -1)], axis=1))
            packed.append(jnp.concatenate([side.reshape(8, -1), tail], axis=1))
        total = self.scatter_small(*packed)[0]
        pairs = total[: 6 * 64].reshape(6, 2, 32)
        mine = jnp.where(lax.axis_index("c") == 0, pairs[:, 0], pairs[:, 1])
        qv_len = qvs[0].size // 8
        qv = total[6 * 64 : 6 * 64 + qv_len].reshape(heads, -1)
        up = total[6 * 64 + qv_len :].reshape(1, -1)
        return list(mine), qv, up

    def block_table(self):
        z, y = lax.axis_index("z"), lax.axis_index("y")
        return [((z + dz) % 4) * 2 + (y + dy) % 2 for dy in (0, 1) for dz in range(4)]

    def enter(self, images, cotangent):
        seq, width = images.shape[2:]
        table = jnp.stack(self.block_table() + [lax.axis_index("x")]).astype(jnp.int32)

        def body(table_ref, a_ref, b_ref, a_out, b_out):
            a_out[...] = a_ref[0, 0]
            b_out[...] = b_ref[0, 0]

        block = width // 8
        in_spec = pl.BlockSpec((1, 1, seq, block), lambda i, t: (t[8], 0, 0, t[i]))
        out_spec = pl.BlockSpec((seq, block), lambda i, t: (0, i))
        shape = jax.ShapeDtypeStruct((seq, width), images.dtype)
        return pl.pallas_call(
            body,
            grid_spec=pltpu.PrefetchScalarGridSpec(
                num_scalar_prefetch=1,
                grid=(8,),
                in_specs=[in_spec, in_spec],
                out_specs=[out_spec, out_spec],
            ),
            out_shape=[shape, shape],
            name="enter",
        )(table, images, cotangent)

    def leave(self, rows, dtype):
        rows = rows.astype(bf16)
        seq, width = rows.shape
        half = width // 2
        block = width // 8
        core = lax.axis_index("c")
        mine = jnp.where(core == 0, rows[:, :half], rows[:, half:])
        near = self.swap(mine, "x")
        far = self.swap(near, "c")
        z, y = lax.axis_index("z"), lax.axis_index("y")
        spots = [
            ((y + yy) % 2) * 4 + (zz + 4 - z) % 4 for zz in range(4) for yy in (0, 1)
        ]
        table = jnp.stack(spots + [lax.axis_index("x"), core]).astype(jnp.int32)

        def body(table_ref, own_ref, near_ref, far_ref, out_ref):
            image, spot = pl.program_id(0), pl.program_id(1)
            is_own = image == table_ref[8]
            is_near = table_ref[spot] // 4 == table_ref[9]

            @pl.when(is_own)
            def _():
                out_ref[0, 0] = own_ref[...].astype(dtype)

            @pl.when(jnp.logical_not(is_own) & is_near)
            def _():
                out_ref[0, 0] = near_ref[...].astype(dtype)

            @pl.when(jnp.logical_not(is_own) & jnp.logical_not(is_near))
            def _():
                out_ref[0, 0] = far_ref[...].astype(dtype)

        half_spec = pl.BlockSpec((seq, block), lambda j, i, t: (0, t[i] % 4))
        return pl.pallas_call(
            body,
            grid_spec=pltpu.PrefetchScalarGridSpec(
                num_scalar_prefetch=1,
                grid=(2, 8),
                in_specs=[
                    pl.BlockSpec((seq, block), lambda j, i, t: (0, t[i])),
                    half_spec,
                    half_spec,
                ],
                out_specs=pl.BlockSpec((1, 1, seq, block), lambda j, i, t: (j, 0, 0, i)),
            ),
            out_shape=jax.ShapeDtypeStruct((2, 1, seq, width), dtype),
            name="leave",
        )(table, rows, near, far)


class PlainPlan:
    axes = ("f", "m", "t")
    fsdp = "f"
    tensor = ("m", "t")

    def mesh(self, mesh):
        shape = (mesh.shape["fsdp"], 2, mesh.shape["tensor"] // 2)
        return Mesh(mesh.devices.reshape(shape), self.axes)

    def swap(self, value):
        return lax.ppermute(value, "m", [(0, 1), (1, 0)])

    def micro(self):
        return lax.axis_index("m")

    def gather_all(self, shards):
        def one(shard):
            own = lax.all_gather(shard, "f", axis=0, tiled=True)
            return own, self.swap(own)

        return (shards[0],) + tuple(one(s) for s in shards[1:])

    def scatter(self, d_side, own, other):
        total = mm_tn(d_side, own) + self.swap(mm_tn(d_side, other).astype(bf16)).astype(f32)
        total = total.astype(bf16)
        return lax.psum_scatter(total, "f", scatter_dimension=0, tiled=True).astype(f32)

    def pair_sum(self, part):
        return lax.psum(part.astype(bf16), "t").astype(f32)

    def pack_small(self, vectors, qv, up):
        full = [lax.all_gather(v, self.axes, axis=0, tiled=True) for v in vectors]
        qv = lax.all_gather(qv, "f", axis=1, tiled=True)
        up = lax.all_gather(up, "f", axis=1, tiled=True)
        return full, (qv, self.swap(qv)), (up, self.swap(up))

    def unpack_small(self, packed, heads, qv_cols, up_cols):
        full, qvs, ups = packed
        return (
            [v.astype(f32) for v in full],
            [q.astype(f32) for q in qvs],
            [u.reshape(-1).astype(f32) for u in ups],
        )

    def small_grads(self, vectors, qvs, ups):
        total = lax.psum(jnp.stack(vectors).astype(bf16), ("f", "m")).astype(f32)
        count = lax.axis_size("f") * lax.axis_size("m") * lax.axis_size("t")
        piece = total.shape[1] // count
        mine = lax.dynamic_slice_in_dim(total, lax.axis_index(self.axes) * piece, piece, 1)

        def reduce(pair):
            both = pair[0] + self.swap(pair[1].astype(bf16)).astype(f32)
            return lax.psum_scatter(
                both.astype(bf16), "f", scatter_dimension=1, tiled=True
            ).astype(f32)

        return list(mine), reduce(qvs), reduce([u.reshape(1, -1) for u in ups])

    def enter(self, images, cotangent):
        index = lax.axis_index("m")
        return [
            lax.dynamic_index_in_dim(v, index, 0, False).reshape(-1, v.shape[-1])
            for v in (images, cotangent)
        ]

    def leave(self, rows, dtype):
        rows = rows.astype(bf16)
        other = self.swap(rows)
        first = lax.axis_index("m") == 0
        both = jnp.stack([jnp.where(first, rows, other), jnp.where(first, other, rows)])
        return both[:, None].astype(dtype)


def norm_stats(values):
    mean = jnp.mean(values, axis=-1, keepdims=True)
    centred = values - mean
    inverse = lax.rsqrt(jnp.mean(centred * centred, axis=-1, keepdims=True) + epsilon)
    return mean, inverse


def norm_back(grad, xhat, inverse, gain):
    scaled = grad * gain
    mean_a = jnp.mean(scaled, axis=-1, keepdims=True)
    mean_b = jnp.mean(scaled * xhat, axis=-1, keepdims=True)
    return inverse * (scaled - mean_a - xhat * mean_b)


def attention_forward(q, k, v, heads, head_dim):
    rows = q.shape[0]
    q, k, v = [t.reshape(rows, heads, head_dim) for t in (q, k, v)]
    scores = jnp.einsum("shd,thd->hst", q, k, preferred_element_type=f32) * head_dim ** (-0.5)
    top = jnp.max(scores, axis=-1, keepdims=True)
    exps = jnp.exp(scores - top)
    total = jnp.sum(exps, axis=-1, keepdims=True)
    low = (exps / total).astype(bf16)
    att = jnp.einsum("hst,thd->shd", low, v, preferred_element_type=f32).astype(bf16)
    return att.reshape(rows, heads * head_dim), top + jnp.log(total)


def attention_backward(q, k, v, lse, grad, heads, head_dim):
    rows = q.shape[0]
    q, k, v, grad = [t.reshape(rows, heads, head_dim) for t in (q, k, v, grad)]
    scale = head_dim ** (-0.5)
    scores = jnp.einsum("shd,thd->hst", q, k, preferred_element_type=f32) * scale
    probs = jnp.exp(scores - lse)
    low = probs.astype(bf16)
    val_grad = jnp.einsum("hst,shd->thd", low, grad, preferred_element_type=f32).astype(bf16)
    prob_grad = jnp.einsum("shd,thd->hst", grad, v, preferred_element_type=f32)
    inner = jnp.sum(prob_grad * probs, axis=-1, keepdims=True)
    score_grad = (probs * (prob_grad - inner)).astype(bf16)
    q_grad = jnp.einsum("hst,thd->shd", score_grad, k, preferred_element_type=f32) * scale
    k_grad = jnp.einsum("hst,shd->thd", score_grad, q, preferred_element_type=f32) * scale
    flat = lambda t: t.astype(bf16).reshape(rows, heads * head_dim)
    return flat(q_grad), flat(k_grad), flat(val_grad)


def shards(
    plan,
    images,
    cotangent,
    ln1_gain,
    ln1_bias,
    qkv_weight,
    qv_bias,
    out_weight,
    out_bias,
    ln2_gain,
    ln2_bias,
    up_weight,
    up_bias,
    down_weight,
    down_bias,
):
    rows_own, heads, triple = qkv_weight.shape
    head_dim = triple // 3
    att_cols = heads * head_dim
    hidden = up_weight.shape[1]

    small = plan.pack_small(
        [ln1_gain, ln1_bias, out_bias, ln2_gain, ln2_bias, down_bias], qv_bias, up_bias
    )
    qkv_rows = (
        qkv_weight.reshape(rows_own, heads, 3, head_dim)
        .transpose(0, 2, 1, 3)
        .reshape(rows_own, 3 * att_cols)
    )
    gathered = plan.gather_all((small, qkv_rows, out_weight.T, up_weight, down_weight.T))
    vectors, qvs, ups = plan.unpack_small(gathered[0], heads, qv_bias.shape[1], up_bias.shape[1])
    gain_one, shift_one, out_shift, gain_two, shift_two, down_shift = vectors
    qkv_mat, out_mat, up_mat, down_mat = [jnp.concatenate(p, axis=1) for p in gathered[1:]]

    picture_low, cot_low = plan.enter(images, cotangent)
    picture = picture_low.astype(f32)
    mean_one, inv_one = norm_stats(picture)
    xhat_one = (picture - mean_one) * inv_one
    normed_one = (xhat_one * gain_one + shift_one).astype(bf16)

    projected = mm(normed_one, qkv_mat)
    n_side = 3 * att_cols
    sides = (projected[:, :n_side], projected[:, n_side:])
    queries = jnp.concatenate(
        [
            (s[:, :att_cols] + b[:, :head_dim].reshape(-1)).astype(bf16)
            for s, b in zip(sides, qvs)
        ],
        axis=1,
    )
    key_rows = jnp.concatenate(
        [s[:, att_cols : 2 * att_cols].astype(bf16) for s in sides], axis=1
    )
    val_rows = jnp.concatenate(
        [
            (s[:, 2 * att_cols :] + b[:, head_dim:].reshape(-1)).astype(bf16)
            for s, b in zip(sides, qvs)
        ],
        axis=1,
    )
    attended, lse = attention_forward(queries, key_rows, val_rows, 2 * heads, head_dim)

    branch = plan.pair_sum(mm_nt(attended, out_mat))
    hidden_res = picture + (branch + out_shift)
    mean_two, inv_two = norm_stats(hidden_res)
    xhat_two = (hidden_res - mean_two) * inv_two
    normed_two = (xhat_two * gain_two + shift_two).astype(bf16)
    pre_act = mm(normed_two, up_mat) + jnp.concatenate(ups)
    cdf = 0.5 * (1.0 + lax.erf(pre_act * (0.5**0.5)))
    activated = (pre_act * cdf).astype(bf16)
    mlp_out = plan.pair_sum(mm_nt(activated, down_mat))
    activations = plan.leave(hidden_res + (mlp_out + down_shift), bf16)

    down_grad = plan.scatter(cot_low, activated[:, :hidden], activated[:, hidden:])
    cot = cot_low.astype(f32)
    down_shift_grad = jnp.sum(cot, axis=0)
    slope = cdf + pre_act * jnp.exp(-0.5 * pre_act * pre_act) * 0.3989422804014327
    grad_pre = (mm(cot_low, down_mat) * slope).astype(bf16)
    up_shift_grad = jnp.sum(grad_pre.astype(f32), axis=0)
    grad_two = plan.pair_sum(mm_nt(grad_pre, up_mat))
    up_grad = plan.scatter(normed_two, grad_pre[:, :hidden], grad_pre[:, hidden:])
    gain_two_grad = jnp.sum(grad_two * xhat_two, axis=0)
    shift_two_grad = jnp.sum(grad_two, axis=0)
    grad_hidden = cot + norm_back(grad_two, xhat_two, inv_two, gain_two)
    grad_branch = grad_hidden.astype(bf16)
    out_shift_grad = jnp.sum(grad_branch.astype(f32), axis=0)
    grad_att = mm(grad_branch, out_mat).astype(bf16)
    out_grad = plan.scatter(grad_branch, attended[:, :att_cols], attended[:, att_cols:])

    q_grad, k_grad, v_grad = attention_backward(
        queries, key_rows, val_rows, lse, grad_att, 2 * heads, head_dim
    )
    grad_sides = [
        jnp.concatenate([g[:, i * att_cols : (i + 1) * att_cols] for g in (q_grad, k_grad, v_grad)], axis=1)
        for i in (0, 1)
    ]
    grad_proj = jnp.concatenate(grad_sides, axis=1)
    grad_one = plan.pair_sum(mm_nt(grad_proj, qkv_mat))
    qkv_grad = plan.scatter(normed_one, *grad_sides)
    q_sum = jnp.sum(q_grad.astype(f32), axis=0).reshape(2, heads, head_dim)
    v_sum = jnp.sum(v_grad.astype(f32), axis=0).reshape(2, heads, head_dim)
    qv_sums = jnp.concatenate([q_sum, v_sum], axis=-1)
    gain_one_grad = jnp.sum(grad_one * xhat_one, axis=0)
    shift_one_grad = jnp.sum(grad_one, axis=0)
    input_grad = plan.leave(grad_hidden + norm_back(grad_one, xhat_one, inv_one, gain_one), f32)

    vector_grads, qv_grad, up_bias_grad = plan.small_grads(
        [gain_one_grad, shift_one_grad, out_shift_grad, gain_two_grad, shift_two_grad, down_shift_grad],
        [qv_sums[0], qv_sums[1]],
        [up_shift_grad[:hidden], up_shift_grad[hidden:]],
    )
    qkv_grad = (
        qkv_grad.reshape(rows_own, 3, heads, head_dim)
        .transpose(0, 2, 1, 3)
        .reshape(rows_own, heads, triple)
    )
    return (
        activations,
        input_grad,
        vector_grads[0],
        vector_grads[1],
        qkv_grad,
        qv_grad,
        out_grad.T,
        vector_grads[2],
        vector_grads[3],
        vector_grads[4],
        up_grad,
        up_bias_grad,
        down_grad.T,
        vector_grads[5],
    )


def solution(mesh):
    torus = mesh.shape["fsdp"] == 8 and mesh.shape["tensor"] == 4
    plan = TorusPlan() if torus else PlainPlan()
    fsdp, tensor = plan.fsdp, plan.tensor
    vec = P(plan.axes)
    rows = P(None, fsdp, None, None)
    split = P(fsdp, tensor)
    flip = P(tensor, fsdp)
    head = P(fsdp, tensor, None)
    return jax.shard_map(
        lambda *args: shards(plan, *args),
        mesh=plan.mesh(mesh),
        in_specs=(rows, rows, vec, vec, head, flip, flip, vec, vec, vec, split, flip, flip, vec),
        out_specs=(rows, rows, vec, vec, head, flip, flip, vec, vec, vec, split, flip, flip, vec),
        check_vma=False,
    )
```

```python
import jax
import jax.numpy as jnp
from jax import lax
from jax.experimental import pallas as pl
from jax.experimental.pallas import tpu as pltpu
from jax.sharding import Mesh, PartitionSpec as P

epsilon = 1e-06
f32 = jnp.float32
bf16 = jnp.bfloat16


def after(value, *tokens):
    return lax.optimization_barrier((value,) + tokens)[0]


def dot(a, b, dims):
    return lax.dot_general(a, b, (dims, ((), ())), preferred_element_type=f32)


def mm(a, b):
    return dot(a, b, ((1,), (0,)))


def mm_nt(a, b):
    return dot(a, b, ((1,), (1,)))


def mm_tn(a, b):
    return dot(a, b, ((0,), (0,)))


class TorusPlan:
    axes = ("z", "y", "x", "c")
    fsdp = ("z", "y")
    tensor = ("x", "c")

    def mesh(self, mesh):
        return Mesh(mesh.devices.reshape(4, 2, 2, 2), self.axes)

    def swap(self, value, axis):
        return lax.ppermute(value, axis, [(0, 1), (1, 0)])

    def from_z(self, value, shift):
        return lax.ppermute(value, "z", [((d + shift) % 4, d) for d in range(4)])

    def micro(self):
        return lax.axis_index("x")

    def stage_z(self, shard):
        return jnp.concatenate([shard] + [self.from_z(shard, s) for s in (1, 2, 3)], axis=0)

    def stage_xy(self, four):
        return self.swap(four, "x"), self.swap(four, "y")

    def stage_diag(self, four, over_x, over_y):
        half = four.shape[0] // 2
        return self.swap(over_x[:half], "y"), self.swap(over_y[half:], "x")

    def join(self, four, over_x, over_y, diag_a, diag_b):
        own = jnp.concatenate([four, over_y], axis=0)
        other = jnp.concatenate([over_x, diag_a, diag_b], axis=0)
        return own, other

    def gather_all(self, shards):
        qkv, out, up, down = shards[1:]
        four_s = self.stage_z(shards[0])
        s_xy = self.stage_xy(four_s)
        small = self.join(four_s, *s_xy, *self.stage_diag(four_s, *s_xy))
        four_q = self.stage_z(qkv)
        q_xy = self.stage_xy(four_q)
        four_o = self.stage_z(after(out, four_q))
        four_u = self.stage_z(after(up, four_q))
        q_diag = self.stage_diag(four_q, *q_xy)
        o_xy = self.stage_xy(after(four_o, *q_xy))
        o_diag = self.stage_diag(four_o, *o_xy)
        four_d = self.stage_z(after(down, four_u))
        u_xy = self.stage_xy(after(four_u, *q_diag))
        u_diag = self.stage_diag(four_u, *u_xy)
        d_xy = self.stage_xy(after(four_d, *u_xy))
        d_diag = self.stage_diag(four_d, *d_xy)
        mats = (
            small,
            self.join(four_q, *q_xy, *q_diag),
            self.join(four_o, *o_xy, *o_diag),
            self.join(four_u, *u_xy, *u_diag),
            self.join(four_d, *d_xy, *d_diag),
        )
        return mats, ((four_u, four_d), u_xy, u_diag + o_diag, d_xy)

    def scatter(self, d_side, own, other, tokens=((), (), ())):
        width = d_side.shape[1]
        q, h = width // 4, width // 2
        first = mm_tn(d_side[:, h : h + q], other).astype(bf16)
        second = mm_tn(d_side[:, h + q :], other).astype(bf16)
        first = after(self.swap(first, "y"), *tokens[0]).astype(f32)
        second = after(self.swap(second, "x"), *tokens[0]).astype(f32)
        part_x = mm_tn(d_side[:, :h], other) + jnp.pad(first, ((0, q), (0, 0)))
        part_y = mm_tn(d_side[:, h:], own) + jnp.pad(second, ((q, 0), (0, 0)))
        part_x = after(self.swap(part_x.astype(bf16), "x"), *tokens[1]).astype(f32)
        part_y = after(self.swap(part_y.astype(bf16), "y"), *tokens[1]).astype(f32)
        total = mm_tn(d_side[:, :h], own) + part_x + part_y
        return self.finish(total, tokens[2])

    def finish(self, total, tokens=()):
        rows = total.shape[0] // 4
        total = total.astype(bf16)
        result = total[:rows].astype(f32)
        for shift in (1, 2, 3):
            piece = total[rows * shift : rows * (shift + 1)]
            result = result + after(self.from_z(piece, 4 - shift), *tokens).astype(f32)
        return result

    def scatter_small(self, own, other):
        own, other = own.astype(bf16), other.astype(bf16)
        first = self.swap(other[4:6], "y").astype(f32)
        second = self.swap(other[6:8], "x").astype(f32)
        part_x = other[:4].astype(f32) + jnp.pad(first, ((0, 2), (0, 0)))
        part_y = own[4:].astype(f32) + jnp.pad(second, ((2, 0), (0, 0)))
        part_x = self.swap(part_x.astype(bf16), "x").astype(f32)
        part_y = self.swap(part_y.astype(bf16), "y").astype(f32)
        return self.finish(own[:4].astype(f32) + part_x + part_y)

    def pair_sum(self, part):
        low = part.astype(bf16)
        return low.astype(f32) + self.swap(low, "c").astype(f32)

    def to_abs(self, value):
        value = value.reshape((2, 4) + value.shape[1:])
        value = jnp.where(lax.axis_index("y") == 0, value, value[::-1])
        double = jnp.concatenate([value, value], axis=1)
        value = lax.dynamic_slice_in_dim(double, (4 - lax.axis_index("z")) % 4, 4, 1)
        value = jnp.swapaxes(value, 0, 1)
        return value.reshape((8,) + value.shape[2:])

    def to_rel(self, value):
        value = jnp.swapaxes(value.reshape((4, 2) + value.shape[1:]), 0, 1)
        value = jnp.where(lax.axis_index("y") == 0, value, value[::-1])
        double = jnp.concatenate([value, value], axis=1)
        value = lax.dynamic_slice_in_dim(double, lax.axis_index("z"), 4, 1)
        return value.reshape((8,) + value.shape[2:])

    def pack_small(self, vectors, qv, up):
        mine = jnp.stack(vectors)[:, None]
        theirs = self.swap(mine, "c")
        at_zero = lax.axis_index("c") == 0
        both = jnp.concatenate(
            [jnp.where(at_zero, mine, theirs), jnp.where(at_zero, theirs, mine)], axis=1
        )
        flat = jnp.concatenate([both.reshape(-1), qv.reshape(-1), up.reshape(-1)])
        return flat.reshape(1, -1)

    def unpack_small(self, pair, heads, qv_cols, up_cols):
        own, other = pair
        count = 6 * 64
        at_zero = lax.axis_index("x") == 0
        low = jnp.where(at_zero, own[:, :count], other[:, :count]).reshape(8, 6, 64)
        high = jnp.where(at_zero, other[:, :count], own[:, :count]).reshape(8, 6, 64)
        vectors = jnp.swapaxes(jnp.concatenate([low, high], axis=2), 0, 1).reshape(6, -1)
        qvs, ups = [], []
        for side in (own, other):
            tail = self.to_abs(side[:, count:])
            qv = tail[:, : heads * qv_cols].reshape(8, heads, qv_cols)
            qvs.append(jnp.swapaxes(qv, 0, 1).reshape(heads, 8 * qv_cols))
            ups.append(tail[:, heads * qv_cols :].reshape(-1))
        return list(vectors.astype(f32)), [q.astype(f32) for q in qvs], [u.astype(f32) for u in ups]

    def small_grads(self, vectors, qvs, ups):
        rows = jnp.swapaxes(jnp.stack(vectors).reshape(6, 8, 128), 0, 1)
        at_zero = lax.axis_index("x") == 0
        sides = (
            jnp.where(at_zero, rows[:, :, :64], rows[:, :, 64:]),
            jnp.where(at_zero, rows[:, :, 64:], rows[:, :, :64]),
        )
        packed = []
        heads = qvs[0].shape[0]
        for side, qv, up in zip(sides, qvs, ups):
            qv_rows = jnp.swapaxes(qv.reshape(heads, 8, -1), 0, 1).reshape(8, -1)
            tail = self.to_rel(jnp.concatenate([qv_rows, up.reshape(8, -1)], axis=1))
            packed.append(jnp.concatenate([side.reshape(8, -1), tail], axis=1))
        total = self.scatter_small(*packed)[0]
        pairs = total[: 6 * 64].reshape(6, 2, 32)
        mine = jnp.where(lax.axis_index("c") == 0, pairs[:, 0], pairs[:, 1])
        qv_len = qvs[0].size // 8
        qv = total[6 * 64 : 6 * 64 + qv_len].reshape(heads, -1)
        up = total[6 * 64 + qv_len :].reshape(1, -1)
        return list(mine), qv, up

    def block_table(self):
        z, y = lax.axis_index("z"), lax.axis_index("y")
        return [((z + dz) % 4) * 2 + (y + dy) % 2 for dy in (0, 1) for dz in range(4)]

    def enter(self, images, cotangent):
        seq, width = images.shape[2:]
        table = jnp.stack(self.block_table() + [lax.axis_index("x")]).astype(jnp.int32)

        def body(table_ref, a_ref, b_ref, a_out, b_out):
            a_out[...] = a_ref[0, 0]
            b_out[...] = b_ref[0, 0]

        block = width // 8
        in_spec = pl.BlockSpec((1, 1, seq, block), lambda i, t: (t[8], 0, 0, t[i]))
        out_spec = pl.BlockSpec((seq, block), lambda i, t: (0, i))
        shape = jax.ShapeDtypeStruct((seq, width), images.dtype)
        return pl.pallas_call(
            body,
            grid_spec=pltpu.PrefetchScalarGridSpec(
                num_scalar_prefetch=1,
                grid=(8,),
                in_specs=[in_spec, in_spec],
                out_specs=[out_spec, out_spec],
            ),
            out_shape=[shape, shape],
            name="enter",
        )(table, images, cotangent)

    def reorder(self, width):
        block = width // 8
        starts = jnp.stack(self.block_table())[:, None] * block
        target = (starts + jnp.arange(block)[None]).reshape(-1)
        return after((target[:, None] == jnp.arange(width)[None]).astype(bf16))

    def leave(self, rows, dtype):
        rows = rows.astype(bf16)
        width = rows.shape[1]
        half = width // 2
        rows = mm(rows, self.reorder(width)).astype(bf16)
        at_zero = lax.axis_index("c") == 0
        near = self.swap(jnp.where(at_zero, rows[:, :half], rows[:, half:]), "x")
        far = self.swap(near, "c")
        other = jnp.concatenate(
            [jnp.where(at_zero, near, far), jnp.where(at_zero, far, near)], axis=1
        )
        first = lax.axis_index("x") == 0
        both = jnp.stack([jnp.where(first, rows, other), jnp.where(first, other, rows)])
        return both[:, None].astype(dtype)


class PlainPlan:
    axes = ("f", "m", "t")
    fsdp = "f"
    tensor = ("m", "t")

    def mesh(self, mesh):
        shape = (mesh.shape["fsdp"], 2, mesh.shape["tensor"] // 2)
        return Mesh(mesh.devices.reshape(shape), self.axes)

    def swap(self, value):
        return lax.ppermute(value, "m", [(0, 1), (1, 0)])

    def micro(self):
        return lax.axis_index("m")

    def gather_all(self, shards):
        def one(shard):
            own = lax.all_gather(shard, "f", axis=0, tiled=True)
            return own, self.swap(own)

        return (shards[0],) + tuple(one(s) for s in shards[1:]), ((),) * 4

    def scatter(self, d_side, own, other, tokens=None):
        total = mm_tn(d_side, own) + self.swap(mm_tn(d_side, other).astype(bf16)).astype(f32)
        total = total.astype(bf16)
        return lax.psum_scatter(total, "f", scatter_dimension=0, tiled=True).astype(f32)

    def pair_sum(self, part):
        return lax.psum(part.astype(bf16), "t").astype(f32)

    def pack_small(self, vectors, qv, up):
        full = [lax.all_gather(v, self.axes, axis=0, tiled=True) for v in vectors]
        qv = lax.all_gather(qv, "f", axis=1, tiled=True)
        up = lax.all_gather(up, "f", axis=1, tiled=True)
        return full, (qv, self.swap(qv)), (up, self.swap(up))

    def unpack_small(self, packed, heads, qv_cols, up_cols):
        full, qvs, ups = packed
        return (
            [v.astype(f32) for v in full],
            [q.astype(f32) for q in qvs],
            [u.reshape(-1).astype(f32) for u in ups],
        )

    def small_grads(self, vectors, qvs, ups):
        total = lax.psum(jnp.stack(vectors).astype(bf16), ("f", "m")).astype(f32)
        count = lax.axis_size("f") * lax.axis_size("m") * lax.axis_size("t")
        piece = total.shape[1] // count
        mine = lax.dynamic_slice_in_dim(total, lax.axis_index(self.axes) * piece, piece, 1)

        def reduce(pair):
            both = pair[0] + self.swap(pair[1].astype(bf16)).astype(f32)
            return lax.psum_scatter(
                both.astype(bf16), "f", scatter_dimension=1, tiled=True
            ).astype(f32)

        return list(mine), reduce(qvs), reduce([u.reshape(1, -1) for u in ups])

    def enter(self, images, cotangent):
        index = lax.axis_index("m")
        return [
            lax.dynamic_index_in_dim(v, index, 0, False).reshape(-1, v.shape[-1])
            for v in (images, cotangent)
        ]

    def leave(self, rows, dtype):
        rows = rows.astype(bf16)
        other = self.swap(rows)
        first = lax.axis_index("m") == 0
        both = jnp.stack([jnp.where(first, rows, other), jnp.where(first, other, rows)])
        return both[:, None].astype(dtype)


def norm_stats(values):
    mean = jnp.mean(values, axis=-1, keepdims=True)
    centred = values - mean
    inverse = lax.rsqrt(jnp.mean(centred * centred, axis=-1, keepdims=True) + epsilon)
    return mean, inverse


def norm_back(grad, xhat, inverse, gain):
    scaled = grad * gain
    mean_a = jnp.mean(scaled, axis=-1, keepdims=True)
    mean_b = jnp.mean(scaled * xhat, axis=-1, keepdims=True)
    return inverse * (scaled - mean_a - xhat * mean_b)


def attention_forward(q, k, v, heads, head_dim):
    rows = q.shape[0]
    q, k, v = [t.reshape(rows, heads, head_dim) for t in (q, k, v)]
    scores = jnp.einsum("shd,thd->hst", q, k, preferred_element_type=f32) * head_dim ** (-0.5)
    top = jnp.max(scores, axis=-1, keepdims=True)
    exps = jnp.exp(scores - top)
    total = jnp.sum(exps, axis=-1, keepdims=True)
    low = (exps / total).astype(bf16)
    att = jnp.einsum("hst,thd->shd", low, v, preferred_element_type=f32).astype(bf16)
    return att.reshape(rows, heads * head_dim), top + jnp.log(total)


def attention_backward(q, k, v, lse, grad, heads, head_dim):
    rows = q.shape[0]
    q, k, v, grad = [t.reshape(rows, heads, head_dim) for t in (q, k, v, grad)]
    scale = head_dim ** (-0.5)
    scores = jnp.einsum("shd,thd->hst", q, k, preferred_element_type=f32) * scale
    probs = jnp.exp(scores - lse)
    low = probs.astype(bf16)
    val_grad = jnp.einsum("hst,shd->thd", low, grad, preferred_element_type=f32).astype(bf16)
    prob_grad = jnp.einsum("shd,thd->hst", grad, v, preferred_element_type=f32)
    inner = jnp.sum(prob_grad * probs, axis=-1, keepdims=True)
    score_grad = (probs * (prob_grad - inner)).astype(bf16)
    q_grad = jnp.einsum("hst,thd->shd", score_grad, k, preferred_element_type=f32) * scale
    k_grad = jnp.einsum("hst,shd->thd", score_grad, q, preferred_element_type=f32) * scale
    flat = lambda t: t.astype(bf16).reshape(rows, heads * head_dim)
    return flat(q_grad), flat(k_grad), flat(val_grad)


def shards(
    plan,
    images,
    cotangent,
    ln1_gain,
    ln1_bias,
    qkv_weight,
    qv_bias,
    out_weight,
    out_bias,
    ln2_gain,
    ln2_bias,
    up_weight,
    up_bias,
    down_weight,
    down_bias,
):
    rows_own, heads, triple = qkv_weight.shape
    head_dim = triple // 3
    att_cols = heads * head_dim
    hidden = up_weight.shape[1]

    small = plan.pack_small(
        [ln1_gain, ln1_bias, out_bias, ln2_gain, ln2_bias, down_bias], qv_bias, up_bias
    )
    qkv_rows = (
        qkv_weight.reshape(rows_own, heads, 3, head_dim)
        .transpose(0, 2, 1, 3)
        .reshape(rows_own, 3 * att_cols)
    )
    gathered, stages = plan.gather_all((small, qkv_rows, out_weight.T, up_weight, down_weight.T))
    vectors, qvs, ups = plan.unpack_small(gathered[0], heads, qv_bias.shape[1], up_bias.shape[1])
    gain_one, shift_one, out_shift, gain_two, shift_two, down_shift = vectors
    qkv_mat, out_mat, up_mat, down_mat = [
        after(jnp.concatenate(p, axis=1)) for p in gathered[1:]
    ]

    picture_low, cot_low = plan.enter(images, cotangent)
    picture = picture_low.astype(f32)
    mean_one, inv_one = norm_stats(picture)
    xhat_one = (picture - mean_one) * inv_one
    normed_one = (xhat_one * gain_one + shift_one).astype(bf16)

    normed_one = after(normed_one, *stages[0])
    projected = mm(normed_one, qkv_mat)
    n_side = 3 * att_cols
    sides = (projected[:, :n_side], projected[:, n_side:])
    queries = jnp.concatenate(
        [
            (s[:, :att_cols] + b[:, :head_dim].reshape(-1)).astype(bf16)
            for s, b in zip(sides, qvs)
        ],
        axis=1,
    )
    key_rows = jnp.concatenate(
        [s[:, att_cols : 2 * att_cols].astype(bf16) for s in sides], axis=1
    )
    val_rows = jnp.concatenate(
        [
            (s[:, 2 * att_cols :] + b[:, head_dim:].reshape(-1)).astype(bf16)
            for s, b in zip(sides, qvs)
        ],
        axis=1,
    )
    queries = after(queries, *stages[1])
    attended, lse = attention_forward(queries, key_rows, val_rows, 2 * heads, head_dim)

    attended = after(attended, *stages[2])
    branch = plan.pair_sum(mm_nt(attended, out_mat))
    hidden_res = after(picture + (branch + out_shift), *stages[3])
    mean_two, inv_two = norm_stats(hidden_res)
    xhat_two = (hidden_res - mean_two) * inv_two
    normed_two = (xhat_two * gain_two + shift_two).astype(bf16)
    pre_act = mm(normed_two, up_mat) + jnp.concatenate(ups)
    cdf = 0.5 * (1.0 + lax.erf(pre_act * (0.5**0.5)))
    slope = cdf + pre_act * jnp.exp(-0.5 * pre_act * pre_act) * 0.3989422804014327
    activated, slope = lax.optimization_barrier(
        ((pre_act * cdf).astype(bf16), slope.astype(bf16))
    )
    grad_pre = (mm(cot_low, down_mat) * slope.astype(f32)).astype(bf16)
    mlp_part = mm_nt(activated, down_mat)
    two_part = mm_nt(grad_pre, up_mat)
    mlp_out = plan.pair_sum(mlp_part)
    grad_two = plan.pair_sum(two_part)
    activations = plan.leave(hidden_res + (mlp_out + down_shift), bf16)

    cot = cot_low.astype(f32)
    down_shift_grad = jnp.sum(cot, axis=0)
    up_shift_grad = jnp.sum(grad_pre.astype(f32), axis=0)
    gain_two_grad = jnp.sum(grad_two * xhat_two, axis=0)
    shift_two_grad = jnp.sum(grad_two, axis=0)
    grad_hidden = cot + norm_back(grad_two, xhat_two, inv_two, gain_two)
    grad_branch = grad_hidden.astype(bf16)
    out_shift_grad = jnp.sum(grad_branch.astype(f32), axis=0)
    grad_att = mm(grad_branch, out_mat).astype(bf16)
    q_grad, k_grad, v_grad = attention_backward(
        queries, key_rows, val_rows, lse, grad_att, 2 * heads, head_dim
    )
    grad_sides = [
        jnp.concatenate([g[:, i * att_cols : (i + 1) * att_cols] for g in (q_grad, k_grad, v_grad)], axis=1)
        for i in (0, 1)
    ]
    grad_proj = jnp.concatenate(grad_sides, axis=1)
    grad_one = plan.pair_sum(mm_nt(grad_proj, qkv_mat))
    down_grad = plan.scatter(
        cot_low,
        activated[:, :hidden],
        activated[:, hidden:],
        ((grad_pre,), (grad_hidden,), (grad_att,)),
    )
    up_grad = plan.scatter(
        normed_two,
        grad_pre[:, :hidden],
        grad_pre[:, hidden:],
        ((grad_hidden,), (v_grad,), (grad_proj,)),
    )
    out_grad = plan.scatter(
        grad_branch,
        attended[:, :att_cols],
        attended[:, att_cols:],
        ((v_grad,), (grad_proj,), (grad_proj,)),
    )
    qkv_grad = plan.scatter(normed_one, *grad_sides)
    q_sum = jnp.sum(q_grad.astype(f32), axis=0).reshape(2, heads, head_dim)
    v_sum = jnp.sum(v_grad.astype(f32), axis=0).reshape(2, heads, head_dim)
    qv_sums = jnp.concatenate([q_sum, v_sum], axis=-1)
    gain_one_grad = jnp.sum(grad_one * xhat_one, axis=0)
    shift_one_grad = jnp.sum(grad_one, axis=0)
    input_grad = plan.leave(grad_hidden + norm_back(grad_one, xhat_one, inv_one, gain_one), f32)

    vector_grads, qv_grad, up_bias_grad = plan.small_grads(
        [gain_one_grad, shift_one_grad, out_shift_grad, gain_two_grad, shift_two_grad, down_shift_grad],
        [qv_sums[0], qv_sums[1]],
        [up_shift_grad[:hidden], up_shift_grad[hidden:]],
    )
    qkv_grad = (
        qkv_grad.reshape(rows_own, 3, heads, head_dim)
        .transpose(0, 2, 1, 3)
        .reshape(rows_own, heads, triple)
    )
    return (
        activations,
        input_grad,
        vector_grads[0],
        vector_grads[1],
        qkv_grad,
        qv_grad,
        out_grad.T,
        vector_grads[2],
        vector_grads[3],
        vector_grads[4],
        up_grad,
        up_bias_grad,
        down_grad.T,
        vector_grads[5],
    )


def solution(mesh):
    torus = mesh.shape["fsdp"] == 8 and mesh.shape["tensor"] == 4
    plan = TorusPlan() if torus else PlainPlan()
    fsdp, tensor = plan.fsdp, plan.tensor
    vec = P(plan.axes)
    rows = P(None, fsdp, None, None)
    split = P(fsdp, tensor)
    flip = P(tensor, fsdp)
    head = P(fsdp, tensor, None)
    return jax.shard_map(
        lambda *args: shards(plan, *args),
        mesh=plan.mesh(mesh),
        in_specs=(rows, rows, vec, vec, head, flip, flip, vec, vec, vec, split, flip, flip, vec),
        out_specs=(rows, rows, vec, vec, head, flip, flip, vec, vec, vec, split, flip, flip, vec),
        check_vma=False,
    )
```

```python
import jax
import jax.numpy as jnp
from jax import lax
from jax.experimental import pallas as pl
from jax.experimental.pallas import tpu as pltpu
from jax.sharding import Mesh, PartitionSpec as P

epsilon = 1e-06
f32 = jnp.float32
bf16 = jnp.bfloat16


def after(value, *tokens):
    return lax.optimization_barrier((value,) + tokens)[0]


def dot(a, b, dims):
    return lax.dot_general(a, b, (dims, ((), ())), preferred_element_type=f32)


def mm(a, b):
    return dot(a, b, ((1,), (0,)))


def mm_nt(a, b):
    return dot(a, b, ((1,), (1,)))


def mm_tn(a, b):
    return dot(a, b, ((0,), (0,)))


class TorusPlan:
    axes = ("z", "y", "x", "c")
    fsdp = ("z", "y")
    tensor = ("x", "c")

    def mesh(self, mesh):
        return Mesh(mesh.devices.reshape(4, 2, 2, 2), self.axes)

    def swap(self, value, axis):
        return lax.ppermute(value, axis, [(0, 1), (1, 0)])

    def from_z(self, value, shift):
        return lax.ppermute(value, "z", [((d + shift) % 4, d) for d in range(4)])

    def micro(self):
        return lax.axis_index("x")

    def stage_z(self, shard):
        return jnp.concatenate([shard] + [self.from_z(shard, s) for s in (1, 2, 3)], axis=0)

    def stage_xy(self, four):
        return self.swap(four, "x"), self.swap(four, "y")

    def stage_diag(self, four, over_x, over_y):
        half = four.shape[0] // 2
        return self.swap(over_x[:half], "y"), self.swap(over_y[half:], "x")

    def join(self, four, over_x, over_y, diag_a, diag_b):
        own = jnp.concatenate([four, over_y], axis=0)
        other = jnp.concatenate([over_x, diag_a, diag_b], axis=0)
        return own, other

    def gather_all(self, shards):
        qkv, out, up, down = shards[1:]
        four_s = self.stage_z(shards[0])
        s_xy = self.stage_xy(four_s)
        small = self.join(four_s, *s_xy, *self.stage_diag(four_s, *s_xy))
        four_q = self.stage_z(qkv)
        q_xy = self.stage_xy(four_q)
        four_o = self.stage_z(after(out, four_q))
        four_u = self.stage_z(after(up, four_q))
        q_diag = self.stage_diag(four_q, *q_xy)
        o_xy = self.stage_xy(after(four_o, *q_xy))
        o_diag = self.stage_diag(four_o, *o_xy)
        four_d = self.stage_z(after(down, four_u))
        u_xy = self.stage_xy(after(four_u, *q_diag))
        u_diag = self.stage_diag(four_u, *u_xy)
        d_xy = self.stage_xy(after(four_d, *u_diag))
        d_diag = self.stage_diag(four_d, *d_xy)
        mats = (
            small,
            self.join(four_q, *q_xy, *q_diag),
            self.join(four_o, *o_xy, *o_diag),
            self.join(four_u, *u_xy, *u_diag),
            self.join(four_d, *d_xy, *d_diag),
        )
        return mats, ((four_u,), u_xy + (four_d,), u_diag + o_diag, d_xy)

    def scatter(self, d_side, own, other, tokens=((), (), ())):
        width = d_side.shape[1]
        q, h = width // 4, width // 2
        first = mm_tn(d_side[:, h : h + q], other).astype(bf16)
        second = mm_tn(d_side[:, h + q :], other).astype(bf16)
        first = after(self.swap(first, "y"), *tokens[0]).astype(f32)
        second = after(self.swap(second, "x"), *tokens[0]).astype(f32)
        part_x = mm_tn(d_side[:, :h], other) + jnp.pad(first, ((0, q), (0, 0)))
        part_y = mm_tn(d_side[:, h:], own) + jnp.pad(second, ((q, 0), (0, 0)))
        part_x = after(self.swap(part_x.astype(bf16), "x"), *tokens[1]).astype(f32)
        part_y = after(self.swap(part_y.astype(bf16), "y"), *tokens[1]).astype(f32)
        total = mm_tn(d_side[:, :h], own) + part_x + part_y
        return self.finish(total, tokens[2])

    def finish(self, total, tokens=()):
        rows = total.shape[0] // 4
        total = total.astype(bf16)
        result = total[:rows].astype(f32)
        for shift in (1, 2, 3):
            piece = total[rows * shift : rows * (shift + 1)]
            result = result + after(self.from_z(piece, 4 - shift), *tokens).astype(f32)
        return result

    def scatter_small(self, own, other):
        own, other = own.astype(bf16), other.astype(bf16)
        first = self.swap(other[4:6], "y").astype(f32)
        second = self.swap(other[6:8], "x").astype(f32)
        part_x = other[:4].astype(f32) + jnp.pad(first, ((0, 2), (0, 0)))
        part_y = own[4:].astype(f32) + jnp.pad(second, ((2, 0), (0, 0)))
        part_x = self.swap(part_x.astype(bf16), "x").astype(f32)
        part_y = self.swap(part_y.astype(bf16), "y").astype(f32)
        return self.finish(own[:4].astype(f32) + part_x + part_y)

    def pair_sum(self, part):
        low = part.astype(bf16)
        return low.astype(f32) + self.swap(low, "c").astype(f32)

    def to_abs(self, value):
        value = value.reshape((2, 4) + value.shape[1:])
        value = jnp.where(lax.axis_index("y") == 0, value, value[::-1])
        double = jnp.concatenate([value, value], axis=1)
        value = lax.dynamic_slice_in_dim(double, (4 - lax.axis_index("z")) % 4, 4, 1)
        value = jnp.swapaxes(value, 0, 1)
        return value.reshape((8,) + value.shape[2:])

    def to_rel(self, value):
        value = jnp.swapaxes(value.reshape((4, 2) + value.shape[1:]), 0, 1)
        value = jnp.where(lax.axis_index("y") == 0, value, value[::-1])
        double = jnp.concatenate([value, value], axis=1)
        value = lax.dynamic_slice_in_dim(double, lax.axis_index("z"), 4, 1)
        return value.reshape((8,) + value.shape[2:])

    def pack_small(self, vectors, qv, up):
        mine = jnp.stack(vectors)[:, None]
        theirs = self.swap(mine, "c")
        at_zero = lax.axis_index("c") == 0
        both = jnp.concatenate(
            [jnp.where(at_zero, mine, theirs), jnp.where(at_zero, theirs, mine)], axis=1
        )
        flat = jnp.concatenate([both.reshape(-1), qv.reshape(-1), up.reshape(-1)])
        return flat.reshape(1, -1)

    def unpack_small(self, pair, heads, qv_cols, up_cols):
        own, other = pair
        count = 6 * 64
        at_zero = lax.axis_index("x") == 0
        low = jnp.where(at_zero, own[:, :count], other[:, :count]).reshape(8, 6, 64)
        high = jnp.where(at_zero, other[:, :count], own[:, :count]).reshape(8, 6, 64)
        vectors = jnp.swapaxes(jnp.concatenate([low, high], axis=2), 0, 1).reshape(6, -1)
        qvs, ups = [], []
        for side in (own, other):
            tail = self.to_abs(side[:, count:])
            qv = tail[:, : heads * qv_cols].reshape(8, heads, qv_cols)
            qvs.append(jnp.swapaxes(qv, 0, 1).reshape(heads, 8 * qv_cols))
            ups.append(tail[:, heads * qv_cols :].reshape(-1))
        return list(vectors.astype(f32)), [q.astype(f32) for q in qvs], [u.astype(f32) for u in ups]

    def small_grads(self, vectors, qvs, ups):
        rows = jnp.swapaxes(jnp.stack(vectors).reshape(6, 8, 128), 0, 1)
        at_zero = lax.axis_index("x") == 0
        sides = (
            jnp.where(at_zero, rows[:, :, :64], rows[:, :, 64:]),
            jnp.where(at_zero, rows[:, :, 64:], rows[:, :, :64]),
        )
        packed = []
        heads = qvs[0].shape[0]
        for side, qv, up in zip(sides, qvs, ups):
            qv_rows = jnp.swapaxes(qv.reshape(heads, 8, -1), 0, 1).reshape(8, -1)
            tail = self.to_rel(jnp.concatenate([qv_rows, up.reshape(8, -1)], axis=1))
            packed.append(jnp.concatenate([side.reshape(8, -1), tail], axis=1))
        total = self.scatter_small(*packed)[0]
        pairs = total[: 6 * 64].reshape(6, 2, 32)
        mine = jnp.where(lax.axis_index("c") == 0, pairs[:, 0], pairs[:, 1])
        qv_len = qvs[0].size // 8
        qv = total[6 * 64 : 6 * 64 + qv_len].reshape(heads, -1)
        up = total[6 * 64 + qv_len :].reshape(1, -1)
        return list(mine), qv, up

    def block_table(self):
        z, y = lax.axis_index("z"), lax.axis_index("y")
        return [((z + dz) % 4) * 2 + (y + dy) % 2 for dy in (0, 1) for dz in range(4)]

    def enter(self, images, cotangent):
        seq, width = images.shape[2:]
        table = jnp.stack(self.block_table() + [lax.axis_index("x")]).astype(jnp.int32)

        def body(table_ref, a_ref, b_ref, a_out, b_out):
            a_out[...] = a_ref[0, 0]
            b_out[...] = b_ref[0, 0]

        block = width // 8
        in_spec = pl.BlockSpec((1, 1, seq, block), lambda i, t: (t[8], 0, 0, t[i]))
        out_spec = pl.BlockSpec((seq, block), lambda i, t: (0, i))
        shape = jax.ShapeDtypeStruct((seq, width), images.dtype)
        return pl.pallas_call(
            body,
            grid_spec=pltpu.PrefetchScalarGridSpec(
                num_scalar_prefetch=1,
                grid=(8,),
                in_specs=[in_spec, in_spec],
                out_specs=[out_spec, out_spec],
            ),
            out_shape=[shape, shape],
            name="enter",
        )(table, images, cotangent)

    def reorder(self, width):
        block = width // 8
        starts = jnp.stack(self.block_table())[:, None] * block
        target = (starts + jnp.arange(block)[None]).reshape(-1)
        return after((target[:, None] == jnp.arange(width)[None]).astype(bf16))

    def leave(self, rows, dtype):
        rows = rows.astype(bf16)
        width = rows.shape[1]
        half = width // 2
        rows = mm(rows, self.reorder(width)).astype(bf16)
        at_zero = lax.axis_index("c") == 0
        near = self.swap(jnp.where(at_zero, rows[:, :half], rows[:, half:]), "x")
        far = self.swap(near, "c")
        other = jnp.concatenate(
            [jnp.where(at_zero, near, far), jnp.where(at_zero, far, near)], axis=1
        )
        first = lax.axis_index("x") == 0
        both = jnp.stack([jnp.where(first, rows, other), jnp.where(first, other, rows)])
        return both[:, None].astype(dtype)


class PlainPlan:
    axes = ("f", "m", "t")
    fsdp = "f"
    tensor = ("m", "t")

    def mesh(self, mesh):
        shape = (mesh.shape["fsdp"], 2, mesh.shape["tensor"] // 2)
        return Mesh(mesh.devices.reshape(shape), self.axes)

    def swap(self, value):
        return lax.ppermute(value, "m", [(0, 1), (1, 0)])

    def micro(self):
        return lax.axis_index("m")

    def gather_all(self, shards):
        def one(shard):
            own = lax.all_gather(shard, "f", axis=0, tiled=True)
            return own, self.swap(own)

        return (shards[0],) + tuple(one(s) for s in shards[1:]), ((),) * 4

    def scatter(self, d_side, own, other, tokens=None):
        total = mm_tn(d_side, own) + self.swap(mm_tn(d_side, other).astype(bf16)).astype(f32)
        total = total.astype(bf16)
        return lax.psum_scatter(total, "f", scatter_dimension=0, tiled=True).astype(f32)

    def pair_sum(self, part):
        return lax.psum(part.astype(bf16), "t").astype(f32)

    def pack_small(self, vectors, qv, up):
        full = [lax.all_gather(v, self.axes, axis=0, tiled=True) for v in vectors]
        qv = lax.all_gather(qv, "f", axis=1, tiled=True)
        up = lax.all_gather(up, "f", axis=1, tiled=True)
        return full, (qv, self.swap(qv)), (up, self.swap(up))

    def unpack_small(self, packed, heads, qv_cols, up_cols):
        full, qvs, ups = packed
        return (
            [v.astype(f32) for v in full],
            [q.astype(f32) for q in qvs],
            [u.reshape(-1).astype(f32) for u in ups],
        )

    def small_grads(self, vectors, qvs, ups):
        total = lax.psum(jnp.stack(vectors).astype(bf16), ("f", "m")).astype(f32)
        count = lax.axis_size("f") * lax.axis_size("m") * lax.axis_size("t")
        piece = total.shape[1] // count
        mine = lax.dynamic_slice_in_dim(total, lax.axis_index(self.axes) * piece, piece, 1)

        def reduce(pair):
            both = pair[0] + self.swap(pair[1].astype(bf16)).astype(f32)
            return lax.psum_scatter(
                both.astype(bf16), "f", scatter_dimension=1, tiled=True
            ).astype(f32)

        return list(mine), reduce(qvs), reduce([u.reshape(1, -1) for u in ups])

    def enter(self, images, cotangent):
        index = lax.axis_index("m")
        return [
            lax.dynamic_index_in_dim(v, index, 0, False).reshape(-1, v.shape[-1])
            for v in (images, cotangent)
        ]

    def leave(self, rows, dtype):
        rows = rows.astype(bf16)
        other = self.swap(rows)
        first = lax.axis_index("m") == 0
        both = jnp.stack([jnp.where(first, rows, other), jnp.where(first, other, rows)])
        return both[:, None].astype(dtype)


def norm_stats(values):
    mean = jnp.mean(values, axis=-1, keepdims=True)
    centred = values - mean
    inverse = lax.rsqrt(jnp.mean(centred * centred, axis=-1, keepdims=True) + epsilon)
    return mean, inverse


def norm_back(grad, xhat, inverse, gain):
    scaled = grad * gain
    mean_a = jnp.mean(scaled, axis=-1, keepdims=True)
    mean_b = jnp.mean(scaled * xhat, axis=-1, keepdims=True)
    return inverse * (scaled - mean_a - xhat * mean_b)


def attention_forward(q, k, v, heads, head_dim):
    rows = q.shape[0]
    q, k, v = [t.reshape(rows, heads, head_dim) for t in (q, k, v)]
    scores = jnp.einsum("shd,thd->hst", q, k, preferred_element_type=f32) * head_dim ** (-0.5)
    top = jnp.max(scores, axis=-1, keepdims=True)
    exps = jnp.exp(scores - top)
    total = jnp.sum(exps, axis=-1, keepdims=True)
    low = (exps / total).astype(bf16)
    att = jnp.einsum("hst,thd->shd", low, v, preferred_element_type=f32).astype(bf16)
    return att.reshape(rows, heads * head_dim), top + jnp.log(total)


def attention_backward(q, k, v, lse, grad, heads, head_dim):
    rows = q.shape[0]
    q, k, v, grad = [t.reshape(rows, heads, head_dim) for t in (q, k, v, grad)]
    scale = head_dim ** (-0.5)
    scores = jnp.einsum("shd,thd->hst", q, k, preferred_element_type=f32) * scale
    probs = jnp.exp(scores - lse)
    low = probs.astype(bf16)
    val_grad = jnp.einsum("hst,shd->thd", low, grad, preferred_element_type=f32).astype(bf16)
    prob_grad = jnp.einsum("shd,thd->hst", grad, v, preferred_element_type=f32)
    inner = jnp.sum(prob_grad * probs, axis=-1, keepdims=True)
    score_grad = (probs * (prob_grad - inner)).astype(bf16)
    q_grad = jnp.einsum("hst,thd->shd", score_grad, k, preferred_element_type=f32) * scale
    k_grad = jnp.einsum("hst,shd->thd", score_grad, q, preferred_element_type=f32) * scale
    flat = lambda t: t.astype(bf16).reshape(rows, heads * head_dim)
    return flat(q_grad), flat(k_grad), flat(val_grad)


def shards(
    plan,
    images,
    cotangent,
    ln1_gain,
    ln1_bias,
    qkv_weight,
    qv_bias,
    out_weight,
    out_bias,
    ln2_gain,
    ln2_bias,
    up_weight,
    up_bias,
    down_weight,
    down_bias,
):
    rows_own, heads, triple = qkv_weight.shape
    head_dim = triple // 3
    att_cols = heads * head_dim
    hidden = up_weight.shape[1]

    small = plan.pack_small(
        [ln1_gain, ln1_bias, out_bias, ln2_gain, ln2_bias, down_bias], qv_bias, up_bias
    )
    qkv_rows = (
        qkv_weight.reshape(rows_own, heads, 3, head_dim)
        .transpose(0, 2, 1, 3)
        .reshape(rows_own, 3 * att_cols)
    )
    gathered, stages = plan.gather_all((small, qkv_rows, out_weight.T, up_weight, down_weight.T))
    vectors, qvs, ups = plan.unpack_small(gathered[0], heads, qv_bias.shape[1], up_bias.shape[1])
    gain_one, shift_one, out_shift, gain_two, shift_two, down_shift = vectors
    qkv_pair = [after(m) for m in gathered[1]]
    out_mat, up_mat, down_mat = [
        after(jnp.concatenate(p, axis=1)) for p in gathered[2:]
    ]

    picture_low, cot_low = plan.enter(images, cotangent)
    picture = picture_low.astype(f32)
    mean_one, inv_one = norm_stats(picture)
    xhat_one = (picture - mean_one) * inv_one
    normed_one = (xhat_one * gain_one + shift_one).astype(bf16)

    normed_one = after(normed_one, *stages[0])
    sides = [mm(normed_one, m) for m in qkv_pair]
    queries = jnp.concatenate(
        [
            (s[:, :att_cols] + b[:, :head_dim].reshape(-1)).astype(bf16)
            for s, b in zip(sides, qvs)
        ],
        axis=1,
    )
    key_rows = jnp.concatenate(
        [s[:, att_cols : 2 * att_cols].astype(bf16) for s in sides], axis=1
    )
    val_rows = jnp.concatenate(
        [
            (s[:, 2 * att_cols :] + b[:, head_dim:].reshape(-1)).astype(bf16)
            for s, b in zip(sides, qvs)
        ],
        axis=1,
    )
    queries = after(queries, *stages[1])
    attended, lse = attention_forward(queries, key_rows, val_rows, 2 * heads, head_dim)

    attended = after(attended, *stages[2])
    branch = plan.pair_sum(mm_nt(attended, out_mat))
    hidden_res = after(picture + (branch + out_shift), *stages[3])
    mean_two, inv_two = norm_stats(hidden_res)
    xhat_two = (hidden_res - mean_two) * inv_two
    normed_two = (xhat_two * gain_two + shift_two).astype(bf16)
    pre_act = mm(normed_two, up_mat) + jnp.concatenate(ups)
    cdf = 0.5 * (1.0 + lax.erf(pre_act * (0.5**0.5)))
    slope = cdf + pre_act * jnp.exp(-0.5 * pre_act * pre_act) * 0.3989422804014327
    activated, slope = lax.optimization_barrier(
        ((pre_act * cdf).astype(bf16), slope.astype(bf16))
    )
    grad_pre = (mm(cot_low, down_mat) * slope.astype(f32)).astype(bf16)
    mlp_part = mm_nt(activated, down_mat)
    two_part = mm_nt(grad_pre, up_mat)
    mlp_out = plan.pair_sum(mlp_part)
    grad_two = plan.pair_sum(two_part)
    activations = plan.leave(hidden_res + (mlp_out + down_shift), bf16)

    cot = cot_low.astype(f32)
    down_shift_grad = jnp.sum(cot, axis=0)
    up_shift_grad = jnp.sum(grad_pre.astype(f32), axis=0)
    gain_two_grad = jnp.sum(grad_two * xhat_two, axis=0)
    shift_two_grad = jnp.sum(grad_two, axis=0)
    grad_hidden = cot + norm_back(grad_two, xhat_two, inv_two, gain_two)
    grad_branch = grad_hidden.astype(bf16)
    out_shift_grad = jnp.sum(grad_branch.astype(f32), axis=0)
    grad_att = mm(grad_branch, out_mat).astype(bf16)
    q_grad, k_grad, v_grad = attention_backward(
        queries, key_rows, val_rows, lse, grad_att, 2 * heads, head_dim
    )
    grad_sides = [
        jnp.concatenate([g[:, i * att_cols : (i + 1) * att_cols] for g in (q_grad, k_grad, v_grad)], axis=1)
        for i in (0, 1)
    ]
    grad_one = plan.pair_sum(mm_nt(grad_sides[0], qkv_pair[0]) + mm_nt(grad_sides[1], qkv_pair[1]))
    down_grad = plan.scatter(
        cot_low,
        activated[:, :hidden],
        activated[:, hidden:],
        ((grad_pre,), (grad_hidden,), (grad_att,)),
    )
    up_grad = plan.scatter(
        normed_two,
        grad_pre[:, :hidden],
        grad_pre[:, hidden:],
        ((grad_hidden,), (v_grad,), (*grad_sides,)),
    )
    out_grad = plan.scatter(
        grad_branch,
        attended[:, :att_cols],
        attended[:, att_cols:],
        ((v_grad,), (*grad_sides,), (*grad_sides,)),
    )
    qkv_grad = plan.scatter(normed_one, *grad_sides)
    q_sum = jnp.sum(q_grad.astype(f32), axis=0).reshape(2, heads, head_dim)
    v_sum = jnp.sum(v_grad.astype(f32), axis=0).reshape(2, heads, head_dim)
    qv_sums = jnp.concatenate([q_sum, v_sum], axis=-1)
    gain_one_grad = jnp.sum(grad_one * xhat_one, axis=0)
    shift_one_grad = jnp.sum(grad_one, axis=0)
    input_grad = plan.leave(grad_hidden + norm_back(grad_one, xhat_one, inv_one, gain_one), f32)

    vector_grads, qv_grad, up_bias_grad = plan.small_grads(
        [gain_one_grad, shift_one_grad, out_shift_grad, gain_two_grad, shift_two_grad, down_shift_grad],
        [qv_sums[0], qv_sums[1]],
        [up_shift_grad[:hidden], up_shift_grad[hidden:]],
    )
    qkv_grad = (
        qkv_grad.reshape(rows_own, 3, heads, head_dim)
        .transpose(0, 2, 1, 3)
        .reshape(rows_own, heads, triple)
    )
    return (
        activations,
        input_grad,
        vector_grads[0],
        vector_grads[1],
        qkv_grad,
        qv_grad,
        out_grad.T,
        vector_grads[2],
        vector_grads[3],
        vector_grads[4],
        up_grad,
        up_bias_grad,
        down_grad.T,
        vector_grads[5],
    )


def solution(mesh):
    torus = mesh.shape["fsdp"] == 8 and mesh.shape["tensor"] == 4
    plan = TorusPlan() if torus else PlainPlan()
    fsdp, tensor = plan.fsdp, plan.tensor
    vec = P(plan.axes)
    rows = P(None, fsdp, None, None)
    split = P(fsdp, tensor)
    flip = P(tensor, fsdp)
    head = P(fsdp, tensor, None)
    return jax.shard_map(
        lambda *args: shards(plan, *args),
        mesh=plan.mesh(mesh),
        in_specs=(rows, rows, vec, vec, head, flip, flip, vec, vec, vec, split, flip, flip, vec),
        out_specs=(rows, rows, vec, vec, head, flip, flip, vec, vec, vec, split, flip, flip, vec),
        check_vma=False,
    )
```
